128 devices in a mesh: dp: 8 (over x, y_hi), mp: 16 (over y_lo, z, core).
Axes of the slice: x: 4, y: 4 (y_hi: 2, y_lo: 2; y = y_hi * 2 + y_lo), z: 4, core: 2. Of those that a mesh axis runs over, the one named last changes fastest.
Arguments:
- tokens_in: bfloat16 [8192, 4096], P('dp', 'mp'), may hold values from -6 to 6
- grad_out: bfloat16 [8192, 14336], P('dp', 'mp'), may hold values from -6 to 6
- old_first: float32 [32, 128, 14336], P(None, ('dp', 'mp')), may hold values from -2 to 2
- old_second: float32 [32, 128, 14336], P(None, ('dp', 'mp')), may hold values from 0.01 to 1
- old_master: float32 [32, 128, 14336], P(None, ('dp', 'mp')), may hold values from -6 to 6
- step_count: int32 [1], replicated, may hold values from 1 to 31
Outputs:
- new_first: float32 [4096, 14336], P('dp', 'mp')
- new_second: float32 [4096, 14336], P('dp', 'mp')
- new_weights: float32 [4096, 14336], P(None, 'mp')
The draws below stay inside these ranges and needn't reach their ends.
All inputs are finite; a program needn't handle non-finite values.
Results may differ from the reference program's by a relative error of at most 0.0003.
Values may be sent and summed in bfloat16 or wider, within the bound.
No kernel may reach another device: no remote copies, remote signals or barrier semaphores. Data moves between devices by JAX's collectives and lax.ppermute only.
A program may use at most 128 MiB of HBM per device.

```python
import math
import jax
import jax.numpy as jnp
from jax import lax

D = 4096
FF = 14336
TOK_DEV = 1024
TOKENS = 8192
OLD_ROWS = 32
DEVICES = 128


def block_scale(own_key, shape, cuts, smallest, largest):
    level, own = 1.0, jax.random.fold_in(own_key, 6)
    for dim, parts in cuts:
        steps = jnp.exp(jax.random.uniform(jax.random.fold_in(own, dim), (parts,), jnp.float32, smallest / len(cuts), largest / len(cuts)))
        level = level * jnp.repeat(steps, shape[dim] // parts).reshape([-1 if axis == dim else 1 for axis in range(len(shape))])
    return level


def gaussian(stream_key, shape, spread, most, split=(), held_as=jnp.bfloat16):
    level = block_scale(stream_key, shape, split, -0.22, 0.18) if split else 1.0
    drawn = jax.random.normal(stream_key, shape, jnp.float32) * spread * level
    return jnp.minimum(jnp.maximum(drawn, -most), most).astype(held_as)


def setup_inputs(seed: int = 0) -> dict:
    splits = jax.random.split(jax.random.key(seed), 7)
    return {
        "tokens_in": gaussian(splits[0], (TOKENS, D), 1.0, 6.0, ((0, 8), (1, 16))),
        "grad_out": gaussian(splits[1], (TOKENS, FF), 1.0, 6.0, ((0, 8), (1, 16))),
        "old_first": gaussian(splits[2], (OLD_ROWS, DEVICES, FF), 0.3, 2.0, ((1, 128),), jnp.float32),
        "old_second": jnp.clip(jnp.exp(math.log(1.0) - 4.6051702 * jax.random.uniform(splits[3], (OLD_ROWS, DEVICES, FF), jnp.float32) ** block_scale(splits[3], (OLD_ROWS, DEVICES, FF), ((1, 128),), -0.2, 0.2)), 0.01, 1.0),
        "old_master": gaussian(splits[4], (OLD_ROWS, DEVICES, FF), 1.0, 6.0, ((1, 128),), jnp.float32),
        "step_count": jax.random.randint(splits[5], (1,), 1, 32).astype(jnp.int32),
    }


def reference(tokens_in, grad_out, old_first, old_second, old_master, step_count):
    first = old_first.reshape(D, FF)
    second = old_second.reshape(D, FF)
    master = old_master.reshape(D, FF)
    grad_scale = 1.0 / jnp.sqrt(jnp.float32(TOKENS))
    group_count = TOKENS // TOK_DEV

    def add_group(total, group):
        start = (group * TOK_DEV).astype(jnp.int32)
        rows_in = lax.dynamic_slice_in_dim(tokens_in, start, TOK_DEV, 0)
        rows_out = lax.dynamic_slice_in_dim(grad_out, start, TOK_DEV, 0)
        partial_value = jnp.dot(rows_in.T, rows_out, preferred_element_type=jnp.float32) * grad_scale
        return (total + partial_value, None)
    grad, _ = lax.scan(add_group, jnp.zeros((D, FF), jnp.float32), jnp.arange(group_count, dtype=jnp.int32))
    new_first = 0.9 * first + 0.1 * grad
    new_second = 0.95 * second + 0.05 * grad * grad
    step_float = step_count[0].astype(jnp.float32)
    correct_one = 1.0 - jnp.power(jnp.float32(0.9), step_float)
    correct_two = 1.0 - jnp.power(jnp.float32(0.95), step_float)
    update = new_first / correct_one / (jnp.sqrt(new_second / correct_two) + 1e-08)
    new_weights = master - 0.02 * (update + 0.1 * master)
    return (new_first, new_second, new_weights)
```

```python
import math

import jax
import jax.numpy as jnp
from jax import lax
from jax.sharding import PartitionSpec as P


X = 4
HALF = 2
FIRST_UNIT = 2.0**14
SECOND_UNIT = 2.0**15
MASTER_UNIT = 2.0**13
REST_UNIT = 2.0**11
GRAD_UNIT = 2.0
WEIGHT_UNIT = 2.0**12


def dp_at(x, yh):
    return (x % X) * HALF + yh


EAST = [(dp_at(x, h), dp_at(x + 1, h)) for x in range(X) for h in range(HALF)]
WEST = [(dp_at(x, h), dp_at(x - 1, h)) for x in range(X) for h in range(HALF)]
ACROSS = [(dp_at(x, h), dp_at(x, 1 - h)) for x in range(X) for h in range(HALF)]


def token_moves():
    moves = []
    for src_x in range(X):
        for yh in range(HALF):
            for mp in range(16):
                yl, z, core = mp // 8, (mp // 2) % 4, mp % 2
                dst_x = 2 * yl + z // 2
                step = (src_x - dst_x) % X
                slot = step * 4 + ((z % 2) ^ yh) * 2 + core
                moves.append((dp_at(src_x, yh) * 16 + mp, dp_at(dst_x, yh) * 16 + slot))
    return moves


def east(value):
    return lax.ppermute(value, "dp", EAST)


def west(value):
    return lax.ppermute(value, "dp", WEST)


def across(value):
    return lax.ppermute(value, "dp", ACROSS)


def local(tokens_in, grad_out, old_first, old_second, old_master, step_count):
    dp_count = lax.axis_size("dp")
    mp_count = lax.axis_size("mp")
    device_total = dp_count * mp_count
    tok_rows = tokens_in.shape[0]
    col_width = grad_out.shape[1]
    grad_scale = 1.0 / math.sqrt(tok_rows * dp_count)
    run_rows = old_first.shape[0] // dp_count
    half = tok_rows // 2
    block = run_rows * device_total

    tokens = lax.ppermute(tokens_in, ("dp", "mp"), token_moves())
    from_west = east(grad_out)
    from_east = west(grad_out)
    tokens = lax.all_gather(tokens, "mp", axis=1, tiled=True)
    far_top = east(from_west[:half])
    far_bottom = west(from_east[half:])

    lead = (old_first * FIRST_UNIT).astype(jnp.float16)
    scaled = old_master * MASTER_UNIT
    high = lax.reduce_precision(scaled, 5, 10)
    units = [
        lead,
        (old_second * SECOND_UNIT).astype(jnp.float16),
        high.astype(jnp.float16),
        ((scaled - high) * REST_UNIT).astype(jnp.float16),
    ]
    parts = [unit.reshape(dp_count, run_rows, mp_count, col_width) for unit in units]
    packed = jnp.concatenate(parts, axis=3).transpose(1, 0, 2, 3)
    packed = packed.reshape(run_rows, device_total, len(units) * col_width)
    moved = lax.all_to_all(packed, ("dp", "mp"), split_axis=1, concat_axis=1, tiled=True)
    moved = [
        moved[:, :, n * col_width : (n + 1) * col_width].astype(jnp.float32).reshape(block, col_width)
        for n in range(len(units))
    ]

    def product(own):
        total = None
        for step, rows, values in (
            (0, slice(None), grad_out),
            (1, slice(None), from_east),
            (3, slice(None), from_west),
            (2, slice(0, half), far_top),
            (2, slice(half, None), far_bottom),
        ):
            start = (step * 4 + own * 2) * 256
            left = tokens[rows, start : start + block]
            dot = lax.dot_general(left, values, (((0,), (0,)), ((), ())), preferred_element_type=jnp.float32)
            total = dot if total is None else total + dot
        return total * grad_scale

    other = across((product(1) * GRAD_UNIT).astype(jnp.float16))
    grad = product(0) + other.astype(jnp.float32) * (1.0 / GRAD_UNIT)
    first = moved[0] * (1.0 / FIRST_UNIT)
    second = moved[1] * (1.0 / SECOND_UNIT)
    master = (moved[2] + moved[3] * (1.0 / REST_UNIT)) * (1.0 / MASTER_UNIT)
    step_float = step_count[0].astype(jnp.float32)
    correct_one = 1.0 - jnp.power(jnp.float32(0.9), step_float)
    correct_two = 1.0 - jnp.power(jnp.float32(0.95), step_float)
    new_first = 0.9 * first + 0.1 * grad
    new_second = 0.95 * second + 0.05 * grad * grad
    update = new_first / correct_one / (jnp.sqrt(new_second / correct_two) + 1e-08)
    new_master = master - 0.02 * (update + 0.1 * master)
    own = lax.optimization_barrier((new_master * WEIGHT_UNIT).astype(jnp.float16))
    mid = block // 2
    west_row = east(own)
    east_row = west(own)
    pair = across(own)
    far_one = east(west_row[:mid])
    far_two = west(east_row[mid:])
    west_pair = east(pair)
    east_pair = west(pair)
    far_pair_one = across(far_one)
    far_pair_two = across(far_two)
    here = lax.axis_index("dp")
    out = jnp.zeros((dp_count * block, col_width), jnp.float32)
    for values, dx, flip, offset in (
        (own, 0, 0, 0),
        (west_row, 3, 0, 0),
        (east_row, 1, 0, 0),
        (pair, 0, 1, 0),
        (far_one, 2, 0, 0),
        (far_two, 2, 0, mid),
        (west_pair, 3, 1, 0),
        (east_pair, 1, 1, 0),
        (far_pair_one, 2, 1, 0),
        (far_pair_two, 2, 1, mid),
    ):
        row = (((here + dx * HALF) & (dp_count - 1)) ^ flip) * block + offset
        out = lax.dynamic_update_slice(out, values.astype(jnp.float32) * (1.0 / WEIGHT_UNIT), (row, 0))
    return (new_first, new_second, out)


def solution(mesh):
    placed = (
        P("dp", "mp"),
        P("dp", "mp"),
        P(None, ("dp", "mp"), None),
        P(None, ("dp", "mp"), None),
        P(None, ("dp", "mp"), None),
        P(),
    )
    return jax.shard_map(
        local,
        mesh=mesh,
        in_specs=placed,
        out_specs=(P("dp", "mp"), P("dp", "mp"), P(None, "mp")),
        check_vma=False,
    )
```

```python
import math

import jax
import jax.numpy as jnp
from jax import lax
from jax.experimental import pallas as pl
from jax.experimental.pallas import tpu as pltpu
from jax.sharding import PartitionSpec as P


X = 4
HALF = 2
FIRST_UNIT = 2.0**14
SECOND_UNIT = 2.0**15
MASTER_UNIT = 2.0**13
REST_UNIT = 2.0**11
GRAD_UNIT = 2.0
WEIGHT_UNIT = 2.0**12


def dp_at(x, yh):
    return (x % X) * HALF + yh


EAST = [(dp_at(x, h), dp_at(x + 1, h)) for x in range(X) for h in range(HALF)]
WEST = [(dp_at(x, h), dp_at(x - 1, h)) for x in range(X) for h in range(HALF)]
ACROSS = [(dp_at(x, h), dp_at(x, 1 - h)) for x in range(X) for h in range(HALF)]


def token_moves():
    moves = []
    for src_x in range(X):
        for yh in range(HALF):
            for mp in range(16):
                yl, z, core = mp // 8, (mp // 2) % 4, mp % 2
                dst_x = 2 * yl + z // 2
                step = (src_x - dst_x) % X
                slot = step * 4 + ((z % 2) ^ yh) * 2 + core
                moves.append((dp_at(src_x, yh) * 16 + mp, dp_at(dst_x, yh) * 16 + slot))
    return moves


def east(value):
    return lax.ppermute(value, "dp", EAST)


def west(value):
    return lax.ppermute(value, "dp", WEST)


def across(value):
    return lax.ppermute(value, "dp", ACROSS)


def place(rows, pieces, out, shape):
    count = len(pieces)

    def body(row_ref, *refs):
        copies = []
        for n in range(count):
            size = pieces[n].shape[0]
            row = pl.multiple_of(row_ref[n], size)
            copies.append(pltpu.make_async_copy(refs[n], refs[-2].at[pl.ds(row, size)], refs[-1].at[n]))
        for copy in copies:
            copy.start()
        for copy in copies:
            copy.wait()

    anywhere = pl.BlockSpec(memory_space=pl.ANY)
    held = [] if out is None else [out]
    return pl.pallas_call(
        body,
        out_shape=jax.ShapeDtypeStruct(shape, jnp.float32),
        in_specs=[
            pl.BlockSpec(memory_space=pltpu.SMEM),
            *[pl.BlockSpec(memory_space=pltpu.VMEM)] * count,
            *[anywhere] * len(held),
        ],
        out_specs=pl.BlockSpec(memory_space=pltpu.HBM),
        scratch_shapes=[pltpu.SemaphoreType.DMA((count,))],
        input_output_aliases={count + 1: 0} if held else {},
    )(rows, *pieces, *held)


def settle(out):
    return pl.pallas_call(
        lambda out_ref, same_ref: None,
        out_shape=jax.ShapeDtypeStruct(out.shape, out.dtype),
        in_specs=[pl.BlockSpec(memory_space=pltpu.HBM)],
        out_specs=pl.BlockSpec(memory_space=pltpu.HBM),
        input_output_aliases={0: 0},
    )(out)


def local(tokens_in, grad_out, old_first, old_second, old_master, step_count):
    dp_count = lax.axis_size("dp")
    mp_count = lax.axis_size("mp")
    device_total = dp_count * mp_count
    tok_rows = tokens_in.shape[0]
    col_width = grad_out.shape[1]
    grad_scale = 1.0 / math.sqrt(tok_rows * dp_count)
    run_rows = old_first.shape[0] // dp_count
    half = tok_rows // 2
    block = run_rows * device_total

    tokens = lax.ppermute(tokens_in, ("dp", "mp"), token_moves())
    west_top = east(grad_out[:half])
    east_bottom = west(grad_out[half:])
    west_bottom = east(grad_out[half:])
    east_top = west(grad_out[:half])
    tokens = lax.all_gather(tokens, "mp", axis=1, tiled=True)
    far_top = east(west_top)
    far_bottom = west(east_bottom)
    far_group = lax.optimization_barrier(jnp.concatenate([far_top, far_bottom]))
    from_west = lax.optimization_barrier(jnp.concatenate([west_top, west_bottom]))
    from_east = lax.optimization_barrier(jnp.concatenate([east_top, east_bottom]))

    flat = [
        lax.optimization_barrier(state.reshape(dp_count * run_rows, -1))
        for state in (old_first, old_second, old_master)
    ]
    lead = (flat[0] * FIRST_UNIT).astype(jnp.float16)
    scaled = flat[2] * MASTER_UNIT
    high = lax.reduce_precision(scaled, 5, 10)
    units = [
        lead,
        (flat[1] * SECOND_UNIT).astype(jnp.float16),
        high.astype(jnp.float16),
        ((scaled - high) * REST_UNIT).astype(jnp.float16),
    ]
    parts = [unit.reshape(dp_count, run_rows, mp_count, col_width) for unit in units]
    packed = jnp.concatenate(parts, axis=3).transpose(1, 0, 2, 3)
    packed = packed.reshape(run_rows, device_total, len(units) * col_width)
    moved = lax.all_to_all(packed, ("dp", "mp"), split_axis=1, concat_axis=1, tiled=True)
    moved = [
        moved[:, :, n * col_width : (n + 1) * col_width].astype(jnp.float32).reshape(block, col_width)
        for n in range(len(units))
    ]

    def product(own):
        total = None
        for step, rows, values in (
            (0, slice(None), grad_out),
            (1, slice(None), from_east),
            (3, slice(None), from_west),
            (2, slice(None), far_group),
        ):
            start = (step * 4 + own * 2) * 256
            left = tokens[rows, start : start + block]
            dot = lax.dot_general(left, values, (((0,), (0,)), ((), ())), preferred_element_type=jnp.float32)
            total = dot if total is None else total + dot
        return total * grad_scale

    other = (product(1) * GRAD_UNIT).astype(jnp.float16)
    other = across(other)
    mine = lax.optimization_barrier(product(0))
    grad = mine + other.astype(jnp.float32) * (1.0 / GRAD_UNIT)
    first = moved[0] * (1.0 / FIRST_UNIT)
    second = moved[1] * (1.0 / SECOND_UNIT)
    master = (moved[2] + moved[3] * (1.0 / REST_UNIT)) * (1.0 / MASTER_UNIT)
    step_float = step_count[0].astype(jnp.float32)
    correct_one = 1.0 - jnp.power(jnp.float32(0.9), step_float)
    correct_two = 1.0 - jnp.power(jnp.float32(0.95), step_float)
    new_first = 0.9 * first + 0.1 * grad
    new_second = 0.95 * second + 0.05 * grad * grad
    update = new_first / correct_one / (jnp.sqrt(new_second / correct_two) + 1e-08)
    new_master = master - 0.02 * (update + 0.1 * master)
    own = lax.optimization_barrier((new_master * WEIGHT_UNIT).astype(jnp.float16))
    mid = block // 2
    west_row = east(own)
    east_row = west(own)
    pair = across(own)
    far_one = east(west_row[:mid])
    far_two = west(east_row[mid:])
    west_pair = east(pair)
    east_pair = west(pair)
    far_pair_one = across(far_one)
    far_pair_two = across(far_two)
    here = lax.axis_index("dp")

    def spot(dx, flip):
        return (((here + dx * HALF) & (dp_count - 1)) ^ flip) * block

    def wide(values):
        return values.astype(jnp.float32) * (1.0 / WEIGHT_UNIT)

    out = place(spot(0, 0)[None], [wide(own)], None, (dp_count * block, col_width))
    for wave in (
        ((west_row, 3, 0, 0), (east_row, 1, 0, 0)),
        ((pair, 0, 1, 0), (far_one, 2, 0, 0), (far_two, 2, 0, mid)),
        ((west_pair, 3, 1, 0), (east_pair, 1, 1, 0)),
        ((far_pair_one, 2, 1, 0), (far_pair_two, 2, 1, mid)),
    ):
        for values, dx, flip, at in wave:
            out = lax.dynamic_update_slice(out, wide(values), (spot(dx, flip) + at, 0))
    out = settle(out)
    return (new_first, new_second, out)


def solution(mesh):
    placed = (
        P("dp", "mp"),
        P("dp", "mp"),
        P(None, ("dp", "mp"), None),
        P(None, ("dp", "mp"), None),
        P(None, ("dp", "mp"), None),
        P(),
    )
    return jax.shard_map(
        local,
        mesh=mesh,
        in_specs=placed,
        out_specs=(P("dp", "mp"), P("dp", "mp"), P(None, "mp")),
        check_vma=False,
    )
```

```python
import math

import jax
import jax.numpy as jnp
from jax import lax
from jax.experimental import pallas as pl
from jax.experimental.pallas import tpu as pltpu
from jax.sharding import PartitionSpec as P


X = 4
HALF = 2
FIRST_UNIT = 2.0**14
SECOND_UNIT = 2.0**15
MASTER_UNIT = 2.0**13
REST_UNIT = 2.0**11
GRAD_UNIT = 2.0
WEIGHT_UNIT = 2.0**12


def dp_at(x, yh):
    return (x % X) * HALF + yh


EAST = [(dp_at(x, h), dp_at(x + 1, h)) for x in range(X) for h in range(HALF)]
WEST = [(dp_at(x, h), dp_at(x - 1, h)) for x in range(X) for h in range(HALF)]
ACROSS = [(dp_at(x, h), dp_at(x, 1 - h)) for x in range(X) for h in range(HALF)]


def token_moves():
    moves = []
    for src_x in range(X):
        for yh in range(HALF):
            for mp in range(16):
                yl, z, core = mp // 8, (mp // 2) % 4, mp % 2
                dst_x = 2 * yl + z // 2
                step = (src_x - dst_x) % X
                slot = step * 4 + ((z % 2) ^ yh) * 2 + core
                moves.append((dp_at(src_x, yh) * 16 + mp, dp_at(dst_x, yh) * 16 + slot))
    return moves


def east(value):
    return lax.ppermute(value, "dp", EAST)


def west(value):
    return lax.ppermute(value, "dp", WEST)


def across(value):
    return lax.ppermute(value, "dp", ACROSS)


def place(rows, pieces, out, shape):
    count = len(pieces)

    def body(row_ref, *refs):
        copies = []
        for n in range(count):
            size = pieces[n].shape[0]
            row = pl.multiple_of(row_ref[n], size)
            copies.append(pltpu.make_async_copy(refs[n], refs[-2].at[pl.ds(row, size)], refs[-1].at[n]))
        for copy in copies:
            copy.start()
        for copy in copies:
            copy.wait()

    anywhere = pl.BlockSpec(memory_space=pl.ANY)
    held = [] if out is None else [out]
    return pl.pallas_call(
        body,
        out_shape=jax.ShapeDtypeStruct(shape, jnp.float32),
        in_specs=[
            pl.BlockSpec(memory_space=pltpu.SMEM),
            *[pl.BlockSpec(memory_space=pltpu.VMEM)] * count,
            *[anywhere] * len(held),
        ],
        out_specs=pl.BlockSpec(memory_space=pltpu.HBM),
        scratch_shapes=[pltpu.SemaphoreType.DMA((count,))],
        input_output_aliases={count + 1: 0} if held else {},
    )(rows, *pieces, *held)


def settle(out):
    return pl.pallas_call(
        lambda out_ref, same_ref: None,
        out_shape=jax.ShapeDtypeStruct(out.shape, out.dtype),
        in_specs=[pl.BlockSpec(memory_space=pltpu.HBM)],
        out_specs=pl.BlockSpec(memory_space=pltpu.HBM),
        input_output_aliases={0: 0},
    )(out)


def local(tokens_in, grad_out, old_first, old_second, old_master, step_count):
    dp_count = lax.axis_size("dp")
    mp_count = lax.axis_size("mp")
    device_total = dp_count * mp_count
    tok_rows = tokens_in.shape[0]
    col_width = grad_out.shape[1]
    grad_scale = 1.0 / math.sqrt(tok_rows * dp_count)
    run_rows = old_first.shape[0] // dp_count
    half = tok_rows // 2
    block = run_rows * device_total

    tokens = lax.ppermute(tokens_in, ("dp", "mp"), token_moves())
    west_top = east(grad_out[:half])
    east_bottom = west(grad_out[half:])
    west_bottom = east(grad_out[half:])
    east_top = west(grad_out[:half])
    tokens = lax.all_gather(tokens, "mp", axis=0, tiled=True)
    tokens = tokens.reshape(X, 4, tok_rows, -1)
    far_top = east(west_top)
    far_bottom = west(east_bottom)
    far_group = lax.optimization_barrier(jnp.concatenate([far_top, far_bottom]))
    from_west = lax.optimization_barrier(jnp.concatenate([west_top, west_bottom]))
    from_east = lax.optimization_barrier(jnp.concatenate([east_top, east_bottom]))

    flat = [
        lax.optimization_barrier(state.reshape(dp_count * run_rows, -1))
        for state in (old_first, old_second, old_master)
    ]
    lead = (flat[0] * FIRST_UNIT).astype(jnp.float16)
    scaled = flat[2] * MASTER_UNIT
    high = lax.reduce_precision(scaled, 5, 10)
    units = [
        lead,
        (flat[1] * SECOND_UNIT).astype(jnp.float16),
        high.astype(jnp.float16),
        ((scaled - high) * REST_UNIT).astype(jnp.float16),
    ]
    parts = [unit.reshape(dp_count, run_rows, mp_count, col_width) for unit in units]
    packed = jnp.concatenate(parts, axis=3).transpose(1, 0, 2, 3)
    packed = packed.reshape(run_rows, device_total, len(units) * col_width)
    moved = lax.all_to_all(packed, ("dp", "mp"), split_axis=1, concat_axis=1, tiled=True)
    moved = [
        moved[:, :, n * col_width : (n + 1) * col_width].astype(jnp.float32).reshape(block, col_width)
        for n in range(len(units))
    ]

    def product(own):
        total = None
        for step, values in ((0, grad_out), (1, from_east), (3, from_west), (2, far_group)):
            left = tokens[step, 2 * own : 2 * own + 2]
            dot = lax.dot_general(left, values, (((1,), (0,)), ((), ())), preferred_element_type=jnp.float32)
            total = dot if total is None else total + dot
        return total.reshape(block, col_width) * grad_scale

    other = (product(1) * GRAD_UNIT).astype(jnp.float16)
    other = across(other)
    mine = lax.optimization_barrier(product(0))
    grad = mine + other.astype(jnp.float32) * (1.0 / GRAD_UNIT)
    first = moved[0] * (1.0 / FIRST_UNIT)
    second = moved[1] * (1.0 / SECOND_UNIT)
    master = (moved[2] + moved[3] * (1.0 / REST_UNIT)) * (1.0 / MASTER_UNIT)
    step_float = step_count[0].astype(jnp.float32)
    correct_one = 1.0 - jnp.power(jnp.float32(0.9), step_float)
    correct_two = 1.0 - jnp.power(jnp.float32(0.95), step_float)
    new_first = 0.9 * first + 0.1 * grad
    new_second = 0.95 * second + 0.05 * grad * grad
    update = new_first / correct_one / (jnp.sqrt(new_second / correct_two) + 1e-08)
    new_master = master - 0.02 * (update + 0.1 * master)
    own = lax.optimization_barrier((new_master * WEIGHT_UNIT).astype(jnp.float16))
    mine, other, first, second, _ = lax.optimization_barrier((mine, other, moved[0], moved[1], own))
    grad = mine + other.astype(jnp.float32) * (1.0 / GRAD_UNIT)
    new_first = 0.9 * (first * (1.0 / FIRST_UNIT)) + 0.1 * grad
    new_second = 0.95 * (second * (1.0 / SECOND_UNIT)) + 0.05 * grad * grad
    mid = block // 2
    west_row = east(own)
    east_row = west(own)
    pair = across(own)
    far_one = east(west_row[:mid])
    far_two = west(east_row[mid:])
    west_pair = east(pair)
    east_pair = west(pair)
    far_pair_one = across(far_one)
    far_pair_two = across(far_two)
    here = lax.axis_index("dp")

    def spot(dx, flip):
        return (((here + dx * HALF) & (dp_count - 1)) ^ flip) * block

    def wide(values):
        return values.astype(jnp.float32) * (1.0 / WEIGHT_UNIT)

    out = place(spot(0, 0)[None], [wide(own)], None, (dp_count * block, col_width))
    for wave in (
        ((west_row, 3, 0, 0), (east_row, 1, 0, 0)),
        ((pair, 0, 1, 0), (far_one, 2, 0, 0), (far_two, 2, 0, mid)),
        ((west_pair, 3, 1, 0), (east_pair, 1, 1, 0)),
        ((far_pair_one, 2, 1, 0), (far_pair_two, 2, 1, mid)),
    ):
        for values, dx, flip, at in wave:
            out = lax.dynamic_update_slice(out, wide(values), (spot(dx, flip) + at, 0))
    out = settle(out)
    return (new_first, new_second, out)


def solution(mesh):
    placed = (
        P("dp", "mp"),
        P("dp", "mp"),
        P(None, ("dp", "mp"), None),
        P(None, ("dp", "mp"), None),
        P(None, ("dp", "mp"), None),
        P(),
    )
    return jax.shard_map(
        local,
        mesh=mesh,
        in_specs=placed,
        out_specs=(P("dp", "mp"), P("dp", "mp"), P(None, "mp")),
        check_vma=False,
    )
```
